512 devices in a mesh: ctx: 64 (over x, z), tp: 8 (over y, core).
Axes of the slice: x: 4, y: 4, z: 16, core: 2. Of those that a mesh axis runs over, the one named last changes fastest.
Arguments:
- projected: bfloat16 [16384, 3, 4096], P('ctx', None, 'tp'), may hold values from -6 to 6
- short_filter: float32 [3, 3, 4096], P(None, None, 'tp'), may hold values from -3 to 3
- residues: float32 [4096, 16], P('tp'), may hold values from -3 to 3
- rates: float32 [4096, 16], P('tp'), may hold values from 3.0517577e-07 to 0.05
- skip_gain: float32 [4096], P('tp'), may hold values from -3 to 3
- out_weight: bfloat16 [4096, 4096], P('tp', 'ctx'), may hold values from -0.09375 to 0.09375
Outputs:
- mixed: bfloat16 [16384, 4096], P('ctx', 'tp')
The draws below stay inside these ranges and needn't reach their ends.
All inputs are finite; a program needn't handle non-finite values.
Results may differ from the reference program's by a relative error of at most 0.019.
Values may be sent and summed in bfloat16 or wider, within the bound.
A program may use at most 64 MiB of HBM per device.

```python
import math
import jax
import jax.numpy as jnp

D = 4096
ORDER = 16
SHORT = 3
TOKENS = 16384
N_TP = 8


def levels(key, dims, cuts, smallest, top_value):
    factor_of = 1.0
    for axis_at, shards_of in cuts:
        draws = jax.random.uniform(jax.random.fold_in(jax.random.fold_in(key, 6), axis_at), (shards_of,), jnp.float32, smallest / len(cuts), top_value / len(cuts))
        factor_of = factor_of * jnp.repeat(jnp.exp(draws), dims[axis_at] // shards_of).reshape((-1,) + (1,) * (len(dims) - 1 - axis_at))
    return factor_of


def normal_values(key, shape, spread, bound, cuts=(), held_as=jnp.bfloat16):
    factor_of = levels(key, shape, cuts, -0.22, 0.18) if cuts else 1.0
    result = jax.random.normal(key, shape, jnp.float32) * spread * factor_of
    return jnp.minimum(jnp.maximum(result, -bound), bound).astype(held_as)


def setup_inputs(seed: int = 0) -> dict:
    key_list = jax.random.split(jax.random.key(seed), 7)
    projected = normal_values(key_list[0], (TOKENS, SHORT, D), 1.0, 6.0, ((0, 64), (2, 8)))
    short_filter = normal_values(key_list[1], (SHORT, SHORT, D), 0.6, 3.0, ((2, 8),), jnp.float32)
    residues = normal_values(key_list[2], (D, ORDER), 0.5, 3.0, ((0, 8),), jnp.float32)
    rates = jnp.clip(jnp.exp(math.log(0.05) - 12.006645658086184 * jax.random.uniform(key_list[3], (D, ORDER), jnp.float32) ** levels(key_list[3], (D, ORDER), ((0, 8),), -0.2, 0.2)), 3.0517577442878974e-07, 0.05)
    skip_gain = normal_values(key_list[4], (D,), 0.5, 3.0, ((0, 8),), jnp.float32)
    out_weight = normal_values(key_list[5], (D, D), D ** -0.5, 0.09375, ((0, 8), (1, 64)))
    return dict(projected=projected, short_filter=short_filter, residues=residues, rates=rates, skip_gain=skip_gain, out_weight=out_weight)


def reference(projected, short_filter, residues, rates, skip_gain, out_weight):
    length = projected.shape[0]
    stream_data = projected.astype(jnp.float32)
    padded = jnp.concatenate([jnp.zeros((2,) + stream_data.shape[1:], jnp.float32), stream_data], axis=0)
    streams = short_filter[0][None] * padded[2:] + short_filter[1][None] * padded[1:-1] + short_filter[2][None] * padded[:-2]
    query_rows = streams[:, 0]
    gated_rows = streams[:, 1] * streams[:, 2]
    mode_coef = residues * jnp.sqrt(-jnp.expm1(-2.0 * rates))
    steps_float = jnp.arange(length).astype(rates.dtype)
    filt = jnp.zeros((length, residues.shape[0]), rates.dtype)
    for mode in range(residues.shape[1]):
        filt = filt + mode_coef[:, mode][None, :] * jnp.exp(-rates[:, mode][None, :] * steps_float[:, None])
    spectrum = jnp.fft.rfft(gated_rows, n=2 * length, axis=0) * jnp.fft.rfft(filt, n=2 * length, axis=0)
    long_out = jnp.fft.irfft(spectrum, n=2 * length, axis=0)[:length]
    long_out = long_out + skip_gain[None, :] * gated_rows
    hidden = (query_rows * long_out).astype(jnp.bfloat16)
    group_width = hidden.shape[1] // N_TP
    summed = jnp.zeros((length, out_weight.shape[1]), jnp.float32)
    for group in range(N_TP):
        lower = group * group_width
        partial_g = jnp.dot(hidden[:, lower:lower + group_width], out_weight[lower:lower + group_width, :], preferred_element_type=jnp.float32).astype(jnp.bfloat16)
        summed = summed + partial_g.astype(jnp.float32)
    return summed.astype(jnp.bfloat16)
```

```python
import functools

import jax
import jax.numpy as jnp
from jax import lax
from jax.experimental import pallas as pl
from jax.experimental.pallas import tpu as pltpu
from jax.sharding import PartitionSpec as P

MESH = pl.DeviceIdType.MESH
F32 = jnp.float32
BF16 = jnp.bfloat16
SUBS = 8


def kernel(
    dims, first_wait, second_wait,
    p_ref, taps_ref, rate_ref, coef_ref, skip_ref, rate_rows_ref, w_ref,
    out_ref,
    gated, query, carry, grow, hid, hidb,
    ends, got_ends, inits, got_inits,
    wall, own, to_pair, from_pair, far, relay_up, relay_dn,
    fin_up, fin_dn, got_up, got_dn,
    sem_e, sem_i, sem_xa, sem_zap, sem_zam, sem_zbp, sem_zbm,
    sem_xbp, sem_xbm, sem_xbr, sem_loc, sem_pair, sem_y,
):
    nx, nz, ny = dims
    n_ctx = nx * nz
    me = lax.axis_index("ctx")
    tp = lax.axis_index("tp")
    x, z = me // nz, me % nz
    y, core = tp // 2, tp % 2
    steps = p_ref.shape[1] - 2
    chans = p_ref.shape[3]
    modes = rate_ref.shape[0]
    groups = chans // 128
    half = 128
    wrows = w_ref.shape[0]
    ra = wrows // 4

    def ctx_id(xx, zz):
        return (lax.rem(xx + nx, nx) * nz + lax.rem(zz + nz, nz), tp)

    def slot(xx, zz):
        return lax.rem(xx + nx, nx) * nz + lax.rem(zz + nz, nz)

    up = (me, lax.rem(y + 1, ny) * 2 + core)
    dn = (me, lax.rem(y + ny - 1, ny) * 2 + core)
    pair = (me, y * 2 + 1 - core)

    barrier = pltpu.get_barrier_semaphore()

    def greet(k, _):
        pl.semaphore_signal(
            barrier, inc=1, device_id=(lax.rem(me + k, n_ctx), tp), device_id_type=MESH
        )
        return 0

    lax.fori_loop(1, n_ctx, greet, 0)
    for other in (up, dn, pair):
        pl.semaphore_signal(barrier, inc=1, device_id=other, device_id_type=MESH)

    mine = pltpu.make_async_copy(w_ref, wall.at[me], sem_loc.at[0])
    mine.start()

    sub = lax.broadcasted_iota(jnp.int32, (SUBS, 128), 0)
    for q in range(groups):
        lanes = pl.ds(q * 128, 128)

        def row(ref, *idx):
            return jnp.broadcast_to(ref[(*idx, pl.ds(0, 1), lanes)], (SUBS, 128))

        taps = [[row(taps_ref, i, s) for i in range(3)] for s in range(3)]
        decay = [jnp.exp(-row(rate_ref, r)) for r in range(modes)]

        def first_pass(j, state):
            def mixed(s):
                t = taps[s]
                return (
                    t[0] * p_ref[s, j + 2, :, lanes]
                    + t[1] * p_ref[s, j + 1, :, lanes]
                    + t[2] * p_ref[s, j, :, lanes]
                )

            value = mixed(1) * mixed(2)
            gated[j, :, lanes] = value
            query[j, :, lanes] = mixed(0)
            return tuple(decay[r] * state[r] + value for r in range(modes))

        zero = jnp.zeros((SUBS, 128), F32)
        state = lax.fori_loop(0, steps, first_pass, (zero,) * modes, unroll=2)
        for r in range(modes):
            rate = row(rate_ref, r)
            total = state[r]
            for gap in (1, 2, 4):
                moved = jnp.where(sub >= gap, pltpu.roll(total, gap, 0), 0.0)
                total = total + jnp.exp(-(float(steps * gap)) * rate) * moved
            ends[r * groups + q] = total[SUBS - 1:, :]
            carry[r, :, lanes] = jnp.where(sub >= 1, pltpu.roll(total, 1, 0), 0.0)
            grow[r, :, lanes] = jnp.exp(-float(steps) * sub.astype(F32) * rate)

    pl.semaphore_wait(barrier, n_ctx - 1 + 3)

    pending = []

    def remote(src, dst, send, recv, dev):
        return pltpu.make_async_remote_copy(
            src_ref=src, dst_ref=dst, send_sem=send, recv_sem=recv,
            device_id=dev, device_id_type=MESH,
        )

    def exchange(src, dst, sems):
        def one(k):
            other = lax.rem(me + k, n_ctx)
            return remote(
                src.at[other], dst.at[me], sems.at[0, k], sems.at[1, k], (other, tp)
            )

        def come(k):
            other = lax.rem(me - k + n_ctx, n_ctx)
            return remote(
                src.at[other], dst.at[other], sems.at[0, k], sems.at[1, k], (other, tp)
            )

        def go(k, _):
            one(k).start()
            return 0

        def done(k, _):
            come(k).wait_recv()
            return 0

        def sent(k, _):
            one(k).wait_send()
            return 0

        return (
            lambda: lax.fori_loop(1, n_ctx, go, 0),
            lambda: lax.fori_loop(1, n_ctx, done, 0),
            lambda: lax.fori_loop(1, n_ctx, sent, 0),
        )

    go_ends, wait_ends, sent_ends = exchange(ends, got_ends, sem_e)
    go_inits, wait_inits, sent_inits = exchange(inits, got_inits, sem_i)
    go_ends()
    got_ends[me] = ends[me]

    lo, hi = pl.ds(0, ra), pl.ds(ra, wrows - ra)

    def w_copy(part, xx, zz, sems, idx, dev, own_src=False):
        at = wall.at[slot(xx, zz), part]
        src = w_ref.at[part] if own_src else at
        return remote(src, at, sems.at[(0, *idx)], sems.at[(1, *idx)], dev)

    def start(copy):
        copy.start()
        pending.append(copy)

    ring = nz // 2
    z_up, z_dn = ctx_id(x, z + 1), ctx_id(x, z - 1)
    x_up, x_dn = ctx_id(x + 1, z), ctx_id(x - 1, z)

    def send_ap(s, dx):
        start(w_copy(lo, x + dx, z - s + 1, sem_zap, (s, dx), z_up, s == 1 and dx == 0))

    def send_am(s, dx):
        start(w_copy(lo, x + dx, z + s - 1, sem_zam, (s, dx), z_dn, s == 1 and dx == 0))

    def send_bp(s):
        start(w_copy(hi, x, z - s + 1, sem_zbp, (s,), z_up, s == 1))

    def send_bm(s):
        start(w_copy(hi, x, z + s - 1, sem_zbm, (s,), z_dn, s == 1))

    def send_bx(e):
        start(w_copy(hi, x, z + e, sem_xbp, (e % nz,), x_up, e == 0))
        start(w_copy(hi, x, z + e, sem_xbm, (e % nz,), x_dn, e == 0))

    def relay_bx(e):
        w_copy(hi, x - 1, z + e, sem_xbp, (e % nz,), x_up).wait_recv()
        w_copy(hi, x + 1, z + e, sem_xbm, (e % nz,), x_dn).wait_recv()
        if e % 2 == 0:
            start(w_copy(hi, x - 1, z + e, sem_xbr, (e % nz,), x_up))
        else:
            start(w_copy(hi, x + 1, z + e, sem_xbr, (e % nz,), x_dn))

    send_ap(1, 0)
    send_am(1, 0)
    send_bp(1)
    send_bm(1)
    for dx in range(1, nx):
        start(w_copy(lo, x, z, sem_xa, (dx,), ctx_id(x + dx, z), True))
    send_bx(0)
    for dx in range(1, nx):
        w_copy(lo, x + dx, z, sem_xa, (nx - dx,), x_up).wait_recv()
        send_ap(1, dx)
        send_am(1, dx)

    def ring_step(s):
        w_copy(hi, x, z - s, sem_zbp, (s,), z_up).wait_recv()
        if s < ring:
            send_bp(s + 1)
        send_bx(-s)
        if s < ring:
            w_copy(hi, x, z + s, sem_zbm, (s,), z_dn).wait_recv()
            if s < ring - 1:
                send_bm(s + 1)
            send_bx(s)
        for dx in range(nx):
            w_copy(lo, x + dx, z - s, sem_zap, (s, dx), z_up).wait_recv()
            if s < ring:
                send_ap(s + 1, dx)
                w_copy(lo, x + dx, z + s, sem_zam, (s, dx), z_dn).wait_recv()
                if s < ring - 1:
                    send_am(s + 1, dx)
        relay_bx(-(s - 1))
        if s > 1:
            relay_bx(s - 1)

    def prefix():
        wait_ends()
        leap = jnp.exp(-float(steps * SUBS) * rate_rows_ref[me])

        def body(p, state):
            inits[p] = state
            return leap * state + got_ends[p]

        lax.fori_loop(0, n_ctx, body, jnp.zeros((1, 128), F32), unroll=4)
        go_inits()
        got_inits[me] = inits[me]

    def finish_conv():
        wait_inits()
        for q in range(groups):
            lanes = pl.ds(q * 128, 128)

            def row(ref, *idx):
                return jnp.broadcast_to(ref[(*idx, pl.ds(0, 1), lanes)], (SUBS, 128))

            decay = [jnp.exp(-row(rate_ref, r)) for r in range(modes)]
            coef = [row(coef_ref, r) for r in range(modes)]
            skip = row(skip_ref)

            def second_pass(j, state):
                value = gated[j, :, lanes]
                after = tuple(decay[r] * state[r] + value for r in range(modes))
                terms = [coef[r] * after[r] for r in range(modes)] + [skip * value]
                while len(terms) > 1:
                    rest = terms[len(terms) // 2 * 2:]
                    terms = [a + b for a, b in zip(terms[::2], terms[1::2])] + rest
                hid[j, :, lanes] = query[j, :, lanes] * terms[0]
                return after

            begin = tuple(
                carry[r, :, lanes]
                + grow[r, :, lanes] * jnp.broadcast_to(got_inits[r * groups + q], (SUBS, 128))
                for r in range(modes)
            )
            lax.fori_loop(0, steps, second_pass, begin, unroll=2)
        hidb[...] = hid[...].reshape(steps * SUBS, chans).astype(BF16)

    for s in range(1, ring + 1):
        if s == first_wait:
            prefix()
        if s == second_wait:
            finish_conv()
        ring_step(s)
    relay_bx(-ring)
    for e in range(nz):
        w_copy(hi, x + 2, z + e, sem_xbr, (e,), x_up).wait_recv()
    mine.wait()

    per = n_ctx // (2 * ny)

    def project(yy, cc):
        at = pl.multiple_of((yy * 2 + cc) * per, per)
        block = wall[pl.ds(at, per)].reshape(per * wrows, chans)
        return lax.dot_general(
            hidb[...], block, (((1,), (1,)), ((), ())), preferred_element_type=F32
        )

    order = [2, 1, ny - 1, 0]

    def pair_copy(i):
        return remote(to_pair.at[i], from_pair.at[i], sem_pair.at[0, i], sem_pair.at[1, i], pair)

    for i, dy in enumerate(order):
        to_pair[i] = project(lax.rem(y + dy, ny), 1 - core).astype(BF16)
        start(pair_copy(i))
    for i, dy in enumerate(order):
        own[i] = project(lax.rem(y + dy, ny), core)

    def top(ref):
        return ref.at[pl.ds(0, half)]

    def bottom(ref):
        return ref.at[pl.ds(half, half)]

    def y_copy(src, dst, k, dev):
        return remote(src, dst, sem_y.at[0, k], sem_y.at[1, k], dev)

    far_up = y_copy(top(far), relay_up, 0, up)
    far_dn = y_copy(bottom(far), relay_dn, 1, dn)
    up_bottom = y_copy(bottom(fin_up), bottom(got_up), 2, up)
    dn_top = y_copy(top(fin_dn), top(got_dn), 3, dn)
    up_top = y_copy(top(fin_up), top(got_up), 4, up)
    dn_bottom = y_copy(bottom(fin_dn), bottom(got_dn), 5, dn)
    hi_rows, lo_rows = pl.ds(0, half), pl.ds(half, half)

    pair_copy(0).wait_recv()
    far[...] = (own[0] + from_pair[0].astype(F32)).astype(BF16)
    start(far_up)
    start(far_dn)
    pair_copy(1).wait_recv()
    fin_up[lo_rows] = (own[1, lo_rows] + from_pair[1, lo_rows].astype(F32)).astype(BF16)
    start(up_bottom)
    pair_copy(2).wait_recv()
    fin_dn[hi_rows] = (own[2, hi_rows] + from_pair[2, hi_rows].astype(F32)).astype(BF16)
    start(dn_top)
    far_up.wait_recv()
    fin_up[hi_rows] = (
        own[1, hi_rows] + from_pair[1, hi_rows].astype(F32) + relay_up[...].astype(F32)
    ).astype(BF16)
    start(up_top)
    far_dn.wait_recv()
    fin_dn[lo_rows] = (
        own[2, lo_rows] + from_pair[2, lo_rows].astype(F32) + relay_dn[...].astype(F32)
    ).astype(BF16)
    start(dn_bottom)
    pair_copy(3).wait_recv()
    own[3] = own[3] + from_pair[3].astype(F32)
    up_bottom.wait_recv()
    dn_top.wait_recv()
    up_top.wait_recv()
    dn_bottom.wait_recv()
    out_ref[...] = (own[3] + got_up[...].astype(F32) + got_dn[...].astype(F32)).astype(BF16)

    sent_ends()
    sent_inits()
    for copy in pending:
        copy.wait_send()


def per_device(dims, projected, short_filter, residues, rates, skip_gain, out_weight):
    nx, nz, ny = dims
    n_ctx = nx * nz
    rows, _, chans = projected.shape
    modes = rates.shape[1]
    steps = rows // SUBS
    groups = chans // 128
    wrows = out_weight.shape[1]
    earlier = lax.ppermute(projected[-2:], "ctx", [(i, i + 1) for i in range(n_ctx - 1)])
    padded = jnp.concatenate([earlier, projected], axis=0)
    windows = jnp.stack([padded[k * steps:k * steps + steps + 2] for k in range(SUBS)], axis=0)
    laid = windows.transpose(2, 1, 0, 3).astype(F32)
    coef = (residues * jnp.sqrt(-jnp.expm1(-2.0 * rates))).T
    rate_t = rates.T
    dma = pltpu.SemaphoreType.DMA
    vm = pltpu.VMEM
    ring = nz // 2
    out = pl.pallas_call(
        functools.partial(kernel, dims, 3, 6),
        out_shape=jax.ShapeDtypeStruct((rows, chans), BF16),
        in_specs=[pl.BlockSpec(memory_space=pltpu.VMEM)] * 7,
        out_specs=pl.BlockSpec(memory_space=pltpu.VMEM),
        scratch_shapes=[
            vm((steps, SUBS, chans), F32),
            vm((steps, SUBS, chans), F32),
            vm((modes, SUBS, chans), F32),
            vm((modes, SUBS, chans), F32),
            vm((steps, SUBS, chans), F32),
            vm((rows, chans), BF16),
            vm((n_ctx, 1, 128), F32),
            vm((n_ctx, 1, 128), F32),
            vm((n_ctx, 1, 128), F32),
            vm((n_ctx, 1, 128), F32),
            vm((n_ctx, wrows, chans), BF16),
            vm((ny, rows, chans), F32),
            vm((ny, rows, chans), BF16),
            vm((ny, rows, chans), BF16),
            vm((rows, chans), BF16),
            vm((rows // 2, chans), BF16),
            vm((rows // 2, chans), BF16),
            vm((rows, chans), BF16),
            vm((rows, chans), BF16),
            vm((rows, chans), BF16),
            vm((rows, chans), BF16),
            dma((2, n_ctx)),
            dma((2, n_ctx)),
            dma((2, nx)),
            dma((2, ring + 1, nx)),
            dma((2, ring + 1, nx)),
            dma((2, ring + 1)),
            dma((2, ring + 1)),
            dma((2, nz)),
            dma((2, nz)),
            dma((2, nz)),
            dma((1,)),
            dma((2, ny)),
            dma((2, 6)),
        ],
        compiler_params=pltpu.CompilerParams(
            collective_id=0, has_side_effects=True, vmem_limit_bytes=48 * 1024 * 1024
        ),
    )(
        laid,
        short_filter[:, :, None, :],
        rate_t[:, None, :],
        coef[:, None, :],
        skip_gain[None, :],
        rate_t.reshape(modes * groups, 1, 128),
        out_weight.T,
    )
    return out.reshape(steps, SUBS, chans).transpose(1, 0, 2).reshape(rows, chans)


def solution(mesh):
    dims = (4, mesh.shape["ctx"] // 4, mesh.shape["tp"] // 2)
    return jax.shard_map(
        functools.partial(per_device, dims),
        mesh=mesh,
        in_specs=(
            P("ctx", None, "tp"),
            P(None, None, "tp"),
            P("tp", None),
            P("tp", None),
            P("tp"),
            P("tp", "ctx"),
        ),
        out_specs=P("ctx", "tp"),
        check_vma=False,
    )
```

```python
import functools

import jax
import jax.numpy as jnp
from jax import lax
from jax.experimental import pallas as pl
from jax.experimental.pallas import tpu as pltpu
from jax.sharding import PartitionSpec as P

MESH = pl.DeviceIdType.MESH
F32 = jnp.float32
BF16 = jnp.bfloat16
SUBS = 8
FIRST, SECOND, SPLIT = 5, 9, 16


def kernel(
    dims, first_wait, second_wait, ra,
    p_in, taps_in, rate_in, res_in, skip_in, w_in,
    out_ref,
    p_ref, taps_ref, rate_ref, res_ref, skip_ref, w_ref,
    pf, tail, coef_ref, leaps, gated, query, carry, grow, hid, hidb,
    ends, got_ends, inits, got_inits,
    wall, own, to_pair, from_pair, far, relay_up, relay_dn,
    fin_up, fin_dn, got_up, got_dn,
    sem_e, sem_i, sem_xa, sem_zap, sem_zam, sem_zbp, sem_zbm,
    sem_xbp, sem_xbm, sem_xbr, sem_loc, sem_pair, sem_y, sem_tail,
    sem_r1, sem_r2, sem_r3, sem_r4,
):
    nx, nz, ny = dims
    n_ctx = nx * nz
    me = lax.axis_index("ctx")
    tp = lax.axis_index("tp")
    x, z = me // nz, me % nz
    y, core = tp // 2, tp % 2
    steps = p_ref.shape[1] // SUBS
    chans = p_ref.shape[2]
    modes = rate_ref.shape[0]
    groups = chans // 128
    half = 128
    wrows = w_ref.shape[0]

    def ctx_id(xx, zz):
        return (lax.rem(xx + nx, nx) * nz + lax.rem(zz + nz, nz), tp)

    def slot(xx, zz):
        return lax.rem(xx + nx, nx) * nz + lax.rem(zz + nz, nz)

    up = (me, lax.rem(y + 1, ny) * 2 + core)
    dn = (me, lax.rem(y + ny - 1, ny) * 2 + core)
    pair = (me, y * 2 + 1 - core)

    loads = [
        pltpu.make_async_copy(src, dst, sem_loc.at[i])
        for i, (src, dst) in enumerate((
            (w_in, w_ref), (p_in, p_ref), (taps_in, taps_ref), (rate_in, rate_ref),
            (res_in, res_ref), (skip_in, skip_ref), (w_in, wall.at[me]),
        ))
    ]
    for load in loads:
        load.start()

    barrier = pltpu.get_barrier_semaphore()

    near = [(lax.rem(x + dx, nx) * nz + z, tp) for dx in range(1, nx)]
    near += [(x * nz + lax.rem(z + dz, nz), tp) for dz in (1, nz - 1)]
    near += [up, dn, pair]
    for other in near:
        pl.semaphore_signal(barrier, inc=1, device_id=other, device_id_type=MESH)

    rows = steps * SUBS
    for load in loads:
        load.wait()
    twice = 2.0 * rate_ref[...]
    small = jnp.ones_like(twice)
    for k in range(9, 1, -1):
        small = 1.0 - small * twice * (1.0 / k)
    lost = jnp.where(twice < 0.25, twice * small, 1.0 - jnp.exp(-twice))
    coef_ref[...] = res_ref[...] * jnp.sqrt(lost)
    for s in range(3):
        for q in range(groups):
            pf[s, q, pl.ds(8, rows), :] = p_ref[s, :, pl.ds(q * 128, 128)].astype(F32)

    pl.semaphore_wait(barrier, len(near))

    pending = []

    def remote(src, dst, send, recv, dev):
        return pltpu.make_async_remote_copy(
            src_ref=src, dst_ref=dst, send_sem=send, recv_sem=recv,
            device_id=dev, device_id_type=MESH,
        )

    def exchange(src, dst, sems):
        def one(k):
            other = lax.rem(me + k, n_ctx)
            return remote(
                src.at[other], dst.at[me], sems.at[0, k], sems.at[1, k], (other, tp)
            )

        def come(k):
            other = lax.rem(me - k + n_ctx, n_ctx)
            return remote(
                src.at[other], dst.at[other], sems.at[0, k], sems.at[1, k], (other, tp)
            )

        def go(k, _):
            one(k).start()
            return 0

        def done(k, _):
            come(k).wait_recv()
            return 0

        def sent(k, _):
            one(k).wait_send()
            return 0

        return (
            lambda: lax.fori_loop(1, n_ctx, go, 0),
            lambda: lax.fori_loop(1, n_ctx, done, 0),
            lambda: lax.fori_loop(1, n_ctx, sent, 0),
        )

    lo, hi = pl.ds(0, ra), pl.ds(ra, wrows - ra)

    def w_copy(part, xx, zz, sems, idx, dev, own_src=False):
        at = wall.at[slot(xx, zz), part]
        src = w_ref.at[part] if own_src else at
        return remote(src, at, sems.at[(0, *idx)], sems.at[(1, *idx)], dev)

    def start(copy):
        copy.start()
        pending.append(copy)

    ring = nz // 2
    z_up, z_dn = ctx_id(x, z + 1), ctx_id(x, z - 1)
    x_up, x_dn = ctx_id(x + 1, z), ctx_id(x - 1, z)

    def send_ap(s, dx):
        start(w_copy(lo, x + dx, z - s + 1, sem_zap, (s, dx), z_up, s == 1 and dx == 0))

    def send_am(s, dx):
        start(w_copy(lo, x + dx, z + s - 1, sem_zam, (s, dx), z_dn, s == 1 and dx == 0))

    def send_bp(s):
        start(w_copy(hi, x, z - s + 1, sem_zbp, (s,), z_up, s == 1))

    def send_bm(s):
        start(w_copy(hi, x, z + s - 1, sem_zbm, (s,), z_dn, s == 1))

    def send_bx(e):
        start(w_copy(hi, x, z + e, sem_xbp, (e % nz,), x_up, e == 0))
        start(w_copy(hi, x, z + e, sem_xbm, (e % nz,), x_dn, e == 0))

    def relay_bx(e):
        w_copy(hi, x - 1, z + e, sem_xbp, (e % nz,), x_up).wait_recv()
        w_copy(hi, x + 1, z + e, sem_xbm, (e % nz,), x_dn).wait_recv()
        if e % 2 == 0:
            start(w_copy(hi, x - 1, z + e, sem_xbr, (e % nz,), x_up))
        else:
            start(w_copy(hi, x + 1, z + e, sem_xbr, (e % nz,), x_dn))

    send_ap(1, 0)
    send_am(1, 0)
    send_bp(1)
    send_bm(1)
    for dx in range(1, nx):
        start(w_copy(lo, x, z, sem_xa, (dx,), ctx_id(x + dx, z), True))
    send_bx(0)
    for dx in range(1, nx):
        w_copy(lo, x + dx, z, sem_xa, (nx - dx,), x_up).wait_recv()
        send_ap(1, dx)
        send_am(1, dx)

    def ring_step(s):
        w_copy(hi, x, z - s, sem_zbp, (s,), z_up).wait_recv()
        if s < ring:
            send_bp(s + 1)
        send_bx(-s)
        if s < ring:
            w_copy(hi, x, z + s, sem_zbm, (s,), z_dn).wait_recv()
            if s < ring - 1:
                send_bm(s + 1)
            send_bx(s)
        for dx in range(nx):
            w_copy(lo, x + dx, z - s, sem_zap, (s, dx), z_up).wait_recv()
            if s < ring:
                send_ap(s + 1, dx)
                w_copy(lo, x + dx, z + s, sem_zam, (s, dx), z_dn).wait_recv()
                if s < ring - 1:
                    send_am(s + 1, dx)
        relay_bx(-(s - 1))
        if s > 1:
            relay_bx(s - 1)

    go_ends, wait_ends, sent_ends = exchange(ends, got_ends, sem_e)
    go_inits, wait_inits, sent_inits = exchange(inits, got_inits, sem_i)


    def herald(sem, gap):
        for dz in (gap, nz - gap):
            pl.semaphore_signal(
                sem, inc=1, device_id=(x * nz + lax.rem(z + dz, nz), tp), device_id_type=MESH
            )

    def row(ref, at, lanes):
        return jnp.broadcast_to(ref[pl.ds(at, 1), lanes], (SUBS, 128))

    sub = lax.broadcasted_iota(jnp.int32, (SUBS, 128), 0)

    def mixer(q):
        lanes = pl.ds(q * 128, 128)
        taps = [
            [jnp.broadcast_to(taps_ref[i, pl.ds(s, 1), lanes], (SUBS, 128)) for i in range(3)]
            for s in range(3)
        ]

        def mixed(s, j):
            return sum(
                taps[s][i] * pf[s, q, pl.ds(8 + j - i, SUBS, stride=steps), :] for i in range(3)
            )

        def at_step(j):
            value = mixed(1, j) * mixed(2, j)
            gated[j, :, lanes] = value
            query[j, :, lanes] = mixed(0, j)
            return value

        return at_step

    def first_pass(q):
        lanes = pl.ds(q * 128, 128)
        decay = [jnp.exp(-row(rate_ref, r, lanes)) for r in range(modes)]
        at_step = mixer(q)

        def body(j, state):
            value = at_step(j)
            return tuple(decay[r] * state[r] + value for r in range(modes))

        zero = jnp.zeros((SUBS, 128), F32)
        state = lax.fori_loop(2, steps, body, (zero,) * modes, unroll=2)
        for r in range(modes):
            carry[r, :, lanes] = state[r]
            grow[r, :, lanes] = jnp.exp(
                -float(steps) * sub.astype(F32) * row(rate_ref, r, lanes)
            )

    def first_steps(q):
        lanes = pl.ds(q * 128, 128)
        for s in range(3):
            edge = tail[s, :, lanes].astype(F32)
            pf[s, q, pl.ds(0, 8), :] = jnp.where(me > 0, edge, 0.0)
        at_step = mixer(q)
        zeroth = at_step(0)
        first = at_step(1)
        for r in range(modes):
            rate = row(rate_ref, r, lanes)
            total = (
                carry[r, :, lanes]
                + jnp.exp(-float(steps - 1) * rate) * zeroth
                + jnp.exp(-float(steps - 2) * rate) * first
            )
            for gap in (1, 2, 4):
                moved = jnp.where(sub >= gap, pltpu.roll(total, gap, 0), 0.0)
                total = total + jnp.exp(-(float(steps * gap)) * rate) * moved
            ends[r * groups + q] = total[SUBS - 1:, :]
            leaps[r * groups + q] = jnp.exp(-float(rows) * rate[:1])
            carry[r, :, lanes] = jnp.where(sub >= 1, pltpu.roll(total, 1, 0), 0.0)

    herald(sem_r1, 1)
    first_pass(0)
    pl.semaphore_wait(sem_r1, 2)
    herald(sem_r2, 2)
    send_tail = remote(
        p_ref.at[:, pl.ds(rows - 8, 8)], tail, sem_tail.at[0], sem_tail.at[1],
        (lax.rem(me + 1, n_ctx), tp),
    )
    start(send_tail)
    first_pass(1)
    pl.semaphore_wait(sem_r2, 2)
    herald(sem_r3, 4)
    for q in range(2, groups):
        first_pass(q)
    send_tail.wait_recv()
    for q in range(groups):
        first_steps(q)
    pl.semaphore_wait(sem_r3, 2)
    herald(sem_r4, 1)

    def depart():
        pl.semaphore_wait(sem_r4, 2)
        go_ends()
        got_ends[me] = ends[me]

    def prefix():
        wait_ends()
        leap = leaps[me]

        def body(p, state):
            inits[p] = state
            return leap * state + got_ends[p]

        lax.fori_loop(0, n_ctx, body, jnp.zeros((1, 128), F32), unroll=4)
        go_inits()
        got_inits[me] = inits[me]

    def finish_conv():
        wait_inits()
        for q in range(groups):
            lanes = pl.ds(q * 128, 128)

            decay = [jnp.exp(-row(rate_ref, r, lanes)) for r in range(modes)]
            coef = [row(coef_ref, r, lanes) for r in range(modes)]
            skip = row(skip_ref, 0, lanes)

            def second_pass(j, state):
                value = gated[j, :, lanes]
                after = tuple(decay[r] * state[r] + value for r in range(modes))
                terms = [coef[r] * after[r] for r in range(modes)] + [skip * value]
                while len(terms) > 1:
                    rest = terms[len(terms) // 2 * 2:]
                    terms = [a + b for a, b in zip(terms[::2], terms[1::2])] + rest
                hid[j, :, lanes] = query[j, :, lanes] * terms[0]
                return after

            begin = tuple(
                carry[r, :, lanes]
                + grow[r, :, lanes] * jnp.broadcast_to(got_inits[r * groups + q], (SUBS, 128))
                for r in range(modes)
            )
            lax.fori_loop(0, steps, second_pass, begin, unroll=2)
        hidb[...] = hid[...].reshape(steps * SUBS, chans).astype(BF16)

    for s in range(1, ring + 2):
        if s == 2:
            depart()
        if s == first_wait:
            prefix()
        if s == second_wait:
            finish_conv()
        if s <= ring:
            ring_step(s)
    relay_bx(-ring)
    for e in range(nz):
        w_copy(hi, x + 2, z + e, sem_xbr, (e,), x_up).wait_recv()

    per = n_ctx // (2 * ny)

    def project(yy, cc):
        at = pl.multiple_of((yy * 2 + cc) * per, per)
        block = wall[pl.ds(at, per)].reshape(per * wrows, chans)
        return lax.dot_general(
            hidb[...], block, (((1,), (1,)), ((), ())), preferred_element_type=F32
        )

    order = [2, 1, ny - 1, 0]

    def pair_copy(i):
        return remote(to_pair.at[i], from_pair.at[i], sem_pair.at[0, i], sem_pair.at[1, i], pair)

    for i, dy in enumerate(order):
        to_pair[i] = project(lax.rem(y + dy, ny), 1 - core).astype(BF16)
        start(pair_copy(i))
    for i, dy in enumerate(order):
        own[i] = project(lax.rem(y + dy, ny), core)

    def top(ref):
        return ref.at[pl.ds(0, half)]

    def bottom(ref):
        return ref.at[pl.ds(half, half)]

    def y_copy(src, dst, k, dev):
        return remote(src, dst, sem_y.at[0, k], sem_y.at[1, k], dev)

    far_up = y_copy(top(far), relay_up, 0, up)
    far_dn = y_copy(bottom(far), relay_dn, 1, dn)
    up_bottom = y_copy(bottom(fin_up), bottom(got_up), 2, up)
    dn_top = y_copy(top(fin_dn), top(got_dn), 3, dn)
    up_top = y_copy(top(fin_up), top(got_up), 4, up)
    dn_bottom = y_copy(bottom(fin_dn), bottom(got_dn), 5, dn)
    hi_rows, lo_rows = pl.ds(0, half), pl.ds(half, half)

    pair_copy(0).wait_recv()
    far[...] = (own[0] + from_pair[0].astype(F32)).astype(BF16)
    start(far_up)
    start(far_dn)
    pair_copy(1).wait_recv()
    fin_up[lo_rows] = (own[1, lo_rows] + from_pair[1, lo_rows].astype(F32)).astype(BF16)
    start(up_bottom)
    pair_copy(2).wait_recv()
    fin_dn[hi_rows] = (own[2, hi_rows] + from_pair[2, hi_rows].astype(F32)).astype(BF16)
    start(dn_top)
    far_up.wait_recv()
    fin_up[hi_rows] = (
        own[1, hi_rows] + from_pair[1, hi_rows].astype(F32) + relay_up[...].astype(F32)
    ).astype(BF16)
    start(up_top)
    far_dn.wait_recv()
    fin_dn[lo_rows] = (
        own[2, lo_rows] + from_pair[2, lo_rows].astype(F32) + relay_dn[...].astype(F32)
    ).astype(BF16)
    start(dn_bottom)
    pair_copy(3).wait_recv()
    own[3] = own[3] + from_pair[3].astype(F32)
    up_bottom.wait_recv()
    dn_top.wait_recv()
    up_top.wait_recv()
    dn_bottom.wait_recv()
    out_ref[...] = (own[3] + got_up[...].astype(F32) + got_dn[...].astype(F32)).astype(BF16)

    sent_ends()
    sent_inits()
    for copy in pending:
        copy.wait_send()


def per_device(dims, projected, short_filter, residues, rates, skip_gain, out_weight):
    nx, nz, ny = dims
    n_ctx = nx * nz
    rows, _, chans = projected.shape
    modes = rates.shape[1]
    steps = rows // SUBS
    groups = chans // 128
    wrows = out_weight.shape[1]
    rate_t = rates.T
    dma = pltpu.SemaphoreType.DMA
    vm = pltpu.VMEM
    ring = nz // 2
    out = pl.pallas_call(
        functools.partial(kernel, dims, FIRST, SECOND, SPLIT),
        out_shape=jax.ShapeDtypeStruct((rows, chans), BF16),
        in_specs=[pl.BlockSpec(memory_space=pltpu.HBM)] * 6,
        out_specs=pl.BlockSpec(memory_space=pltpu.VMEM),
        scratch_shapes=[
            vm((3, rows, chans), BF16),
            vm((3, 3, chans), F32),
            vm((modes, chans), F32),
            vm((modes, chans), F32),
            vm((1, chans), F32),
            vm((wrows, chans), BF16),
            vm((3, groups, rows + 8, 128), F32),
            vm((3, 8, chans), BF16),
            vm((modes, chans), F32),
            vm((n_ctx, 1, 128), F32),
            vm((steps, SUBS, chans), F32),
            vm((steps, SUBS, chans), F32),
            vm((modes, SUBS, chans), F32),
            vm((modes, SUBS, chans), F32),
            vm((steps, SUBS, chans), F32),
            vm((rows, chans), BF16),
            vm((n_ctx, 1, 128), F32),
            vm((n_ctx, 1, 128), F32),
            vm((n_ctx, 1, 128), F32),
            vm((n_ctx, 1, 128), F32),
            vm((n_ctx, wrows, chans), BF16),
            vm((ny, rows, chans), F32),
            vm((ny, rows, chans), BF16),
            vm((ny, rows, chans), BF16),
            vm((rows, chans), BF16),
            vm((rows // 2, chans), BF16),
            vm((rows // 2, chans), BF16),
            vm((rows, chans), BF16),
            vm((rows, chans), BF16),
            vm((rows, chans), BF16),
            vm((rows, chans), BF16),
            dma((2, n_ctx)),
            dma((2, n_ctx)),
            dma((2, nx)),
            dma((2, ring + 1, nx)),
            dma((2, ring + 1, nx)),
            dma((2, ring + 1)),
            dma((2, ring + 1)),
            dma((2, nz)),
            dma((2, nz)),
            dma((2, nz)),
            dma((7,)),
            dma((2, ny)),
            dma((2, 6)),
            dma((2,)),
            pltpu.SemaphoreType.REGULAR,
            pltpu.SemaphoreType.REGULAR,
            pltpu.SemaphoreType.REGULAR,
            pltpu.SemaphoreType.REGULAR,
        ],
        compiler_params=pltpu.CompilerParams(
            collective_id=0, has_side_effects=True, vmem_limit_bytes=67043328
        ),
    )(
        projected.transpose(1, 0, 2),
        short_filter,
        rate_t,
        residues.T,
        skip_gain[None, :],
        out_weight.T,
    )
    return out.reshape(steps, SUBS, chans).transpose(1, 0, 2).reshape(rows, chans)


def solution(mesh):
    dims = (4, mesh.shape["ctx"] // 4, mesh.shape["tp"] // 2)
    return jax.shard_map(
        functools.partial(per_device, dims),
        mesh=mesh,
        in_specs=(
            P("ctx", None, "tp"),
            P(None, None, "tp"),
            P("tp", None),
            P("tp", None),
            P("tp"),
            P("tp", "ctx"),
        ),
        out_specs=P("ctx", "tp"),
        check_vma=False,
    )
```

```python
import functools

import jax
import jax.numpy as jnp
from jax import lax
from jax.experimental import pallas as pl
from jax.experimental.pallas import tpu as pltpu
from jax.sharding import PartitionSpec as P

MESH = pl.DeviceIdType.MESH
F32 = jnp.float32
BF16 = jnp.bfloat16
SUBS = 8
FIRST, SECOND, SPLIT = 6, 9, 16


def kernel(
    dims, first_wait, second_wait, ra,
    p_in, taps_in, rate_in, res_in, skip_in, w_in,
    out_ref,
    p_ref, taps_ref, rate_ref, res_ref, skip_ref, w_ref,
    pf, tail, coef_ref, leaps, gated, query, carry, grow, hid, hidb,
    ends, got_ends, inits, got_inits,
    wall, own, to_pair, from_pair, far, relay_up, relay_dn,
    fin_up, fin_dn, got_up, got_dn,
    sem_e, sem_i, sem_xa, sem_zap, sem_zam, sem_zbp, sem_zbm,
    sem_xbp, sem_xbm, sem_xbr, sem_loc, sem_pair, sem_y, sem_tail,
    sem_r1, sem_r2, sem_r3, sem_r4,
):
    nx, nz, ny = dims
    n_ctx = nx * nz
    me = lax.axis_index("ctx")
    tp = lax.axis_index("tp")
    x, z = me // nz, me % nz
    y, core = tp // 2, tp % 2
    steps = p_ref.shape[1] // SUBS
    chans = p_ref.shape[2]
    modes = rate_ref.shape[0]
    groups = chans // 128
    half = 128
    wrows = w_ref.shape[0]

    def ctx_id(xx, zz):
        return (lax.rem(xx + nx, nx) * nz + lax.rem(zz + nz, nz), tp)

    def slot(xx, zz):
        return lax.rem(xx + nx, nx) * nz + lax.rem(zz + nz, nz)

    up = (me, lax.rem(y + 1, ny) * 2 + core)
    dn = (me, lax.rem(y + ny - 1, ny) * 2 + core)
    pair = (me, y * 2 + 1 - core)

    loads = [
        pltpu.make_async_copy(src, dst, sem_loc.at[i])
        for i, (src, dst) in enumerate((
            (w_in, w_ref), (p_in, p_ref), (taps_in, taps_ref), (rate_in, rate_ref),
            (res_in, res_ref), (skip_in, skip_ref), (w_in, wall.at[me]),
        ))
    ]
    for load in loads:
        load.start()

    barrier = pltpu.get_barrier_semaphore()

    near = [(lax.rem(x + dx, nx) * nz + z, tp) for dx in range(1, nx)]
    near += [(x * nz + lax.rem(z + dz, nz), tp) for dz in (1, nz - 1)]
    near += [up, dn, pair]
    for other in near:
        pl.semaphore_signal(barrier, inc=1, device_id=other, device_id_type=MESH)

    rows = steps * SUBS
    for load in loads:
        load.wait()
    twice = 2.0 * rate_ref[...]
    small = jnp.ones_like(twice)
    for k in range(9, 1, -1):
        small = 1.0 - small * twice * (1.0 / k)
    lost = jnp.where(twice < 0.25, twice * small, 1.0 - jnp.exp(-twice))
    coef_ref[...] = res_ref[...] * jnp.sqrt(lost)
    for s in range(3):
        for q in range(groups):
            pf[s, q, pl.ds(8, rows), :] = p_ref[s, :, pl.ds(q * 128, 128)].astype(F32)

    pl.semaphore_wait(barrier, len(near))

    pending = []

    def remote(src, dst, send, recv, dev):
        return pltpu.make_async_remote_copy(
            src_ref=src, dst_ref=dst, send_sem=send, recv_sem=recv,
            device_id=dev, device_id_type=MESH,
        )

    def exchange(src, dst, sems):
        def one(k):
            other = lax.rem(me + k, n_ctx)
            return remote(
                src.at[other], dst.at[me], sems.at[0, k], sems.at[1, k], (other, tp)
            )

        def come(k):
            other = lax.rem(me - k + n_ctx, n_ctx)
            return remote(
                src.at[other], dst.at[other], sems.at[0, k], sems.at[1, k], (other, tp)
            )

        def go(k, _):
            one(k).start()
            return 0

        def done(k, _):
            come(k).wait_recv()
            return 0

        def sent(k, _):
            one(k).wait_send()
            return 0

        return (
            lambda: lax.fori_loop(1, n_ctx, go, 0),
            lambda: lax.fori_loop(1, n_ctx, done, 0),
            lambda: lax.fori_loop(1, n_ctx, sent, 0),
        )

    lo, hi = pl.ds(0, ra), pl.ds(ra, wrows - ra)

    def w_copy(part, xx, zz, sems, idx, dev, own_src=False):
        at = wall.at[slot(xx, zz), part]
        src = w_ref.at[part] if own_src else at
        return remote(src, at, sems.at[(0, *idx)], sems.at[(1, *idx)], dev)

    def start(copy):
        copy.start()
        pending.append(copy)

    ring = nz // 2
    z_up, z_dn = ctx_id(x, z + 1), ctx_id(x, z - 1)
    x_up, x_dn = ctx_id(x + 1, z), ctx_id(x - 1, z)

    def send_ap(s, dx):
        start(w_copy(lo, x + dx, z - s + 1, sem_zap, (s, dx), z_up, s == 1 and dx == 0))

    def send_am(s, dx):
        start(w_copy(lo, x + dx, z + s - 1, sem_zam, (s, dx), z_dn, s == 1 and dx == 0))

    def send_bp(s):
        start(w_copy(hi, x, z - s + 1, sem_zbp, (s,), z_up, s == 1))

    def send_bm(s):
        start(w_copy(hi, x, z + s - 1, sem_zbm, (s,), z_dn, s == 1))

    def send_bx(e):
        start(w_copy(hi, x, z + e, sem_xbp, (e % nz,), x_up, e == 0))
        start(w_copy(hi, x, z + e, sem_xbm, (e % nz,), x_dn, e == 0))

    def relay_bx(e):
        w_copy(hi, x - 1, z + e, sem_xbp, (e % nz,), x_up).wait_recv()
        w_copy(hi, x + 1, z + e, sem_xbm, (e % nz,), x_dn).wait_recv()
        if e % 2 == 0:
            start(w_copy(hi, x - 1, z + e, sem_xbr, (e % nz,), x_up))
        else:
            start(w_copy(hi, x + 1, z + e, sem_xbr, (e % nz,), x_dn))

    send_ap(1, 0)
    send_am(1, 0)
    send_bp(1)
    send_bm(1)
    for dx in range(1, nx):
        start(w_copy(lo, x, z, sem_xa, (dx,), ctx_id(x + dx, z), True))
    send_bx(0)
    for dx in range(1, nx):
        w_copy(lo, x + dx, z, sem_xa, (nx - dx,), x_up).wait_recv()
        send_ap(1, dx)
        send_am(1, dx)

    def ring_step(s):
        w_copy(hi, x, z - s, sem_zbp, (s,), z_up).wait_recv()
        if s < ring:
            send_bp(s + 1)
        send_bx(-s)
        if s < ring:
            w_copy(hi, x, z + s, sem_zbm, (s,), z_dn).wait_recv()
            if s < ring - 1:
                send_bm(s + 1)
            send_bx(s)
        for dx in range(nx):
            w_copy(lo, x + dx, z - s, sem_zap, (s, dx), z_up).wait_recv()
            if s < ring:
                send_ap(s + 1, dx)
                w_copy(lo, x + dx, z + s, sem_zam, (s, dx), z_dn).wait_recv()
                if s < ring - 1:
                    send_am(s + 1, dx)
        relay_bx(-(s - 1))
        if s > 1:
            relay_bx(s - 1)

    go_ends, wait_ends, sent_ends = exchange(ends, got_ends, sem_e)
    go_inits, wait_inits, sent_inits = exchange(inits, got_inits, sem_i)


    def herald(sem, gap):
        for dz in (gap, nz - gap):
            pl.semaphore_signal(
                sem, inc=1, device_id=(x * nz + lax.rem(z + dz, nz), tp), device_id_type=MESH
            )

    def row(ref, at, lanes):
        return jnp.broadcast_to(ref[pl.ds(at, 1), lanes], (SUBS, 128))

    sub = lax.broadcasted_iota(jnp.int32, (SUBS, 128), 0)

    def lanes_of(q):
        return pl.ds(q * 128 if isinstance(q, int) else pl.multiple_of(q * 128, 128), 128)

    def mixer(q):
        lanes = lanes_of(q)
        taps = [
            [jnp.broadcast_to(taps_ref[i, pl.ds(s, 1), lanes], (SUBS, 128)) for i in range(3)]
            for s in range(3)
        ]

        def load(j):
            return tuple(pf[s, q, pl.ds(8 + j, SUBS, stride=steps), :] for s in range(3))

        def at_step(j, now, last, older):
            mixed = [
                taps[s][0] * now[s] + taps[s][1] * last[s] + taps[s][2] * older[s]
                for s in range(3)
            ]
            value = mixed[1] * mixed[2]
            gated[j, :, lanes] = value
            query[j, :, lanes] = mixed[0]
            return value

        return load, at_step

    def first_pass(q):
        lanes = pl.ds(q * 128, 128)
        decay = [jnp.exp(-row(rate_ref, r, lanes)) for r in range(modes)]
        load, at_step = mixer(q)

        def body(j, held):
            state, last, older = held
            now = load(j)
            value = at_step(j, now, last, older)
            return tuple(decay[r] * state[r] + value for r in range(modes)), now, last

        zero = jnp.zeros((SUBS, 128), F32)
        state, _, _ = lax.fori_loop(2, steps, body, ((zero,) * modes, load(1), load(0)), unroll=2)
        for r in range(modes):
            carry[r, :, lanes] = state[r]
            grow[r, :, lanes] = jnp.exp(
                -float(steps) * sub.astype(F32) * row(rate_ref, r, lanes)
            )

    def first_steps(q, _):
        lanes = lanes_of(q)
        for s in range(3):
            edge = tail[s, :, lanes].astype(F32)
            pf[s, q, pl.ds(0, 8), :] = jnp.where(me > 0, edge, 0.0)
        load, at_step = mixer(q)
        before = [load(j) for j in (-2, -1, 0, 1)]
        zeroth = at_step(0, before[2], before[1], before[0])
        first = at_step(1, before[3], before[2], before[1])
        for r in range(modes):
            rate = row(rate_ref, r, lanes)
            total = (
                carry[r, :, lanes]
                + jnp.exp(-float(steps - 1) * rate) * zeroth
                + jnp.exp(-float(steps - 2) * rate) * first
            )
            for gap in (1, 2, 4):
                moved = jnp.where(sub >= gap, pltpu.roll(total, gap, 0), 0.0)
                total = total + jnp.exp(-(float(steps * gap)) * rate) * moved
            ends[r * groups + q] = total[SUBS - 1:, :]
            leaps[r * groups + q] = jnp.exp(-float(rows) * rate[:1])
            carry[r, :, lanes] = jnp.where(sub >= 1, pltpu.roll(total, 1, 0), 0.0)
        return 0

    def depart():
        pl.semaphore_wait(sem_r4, 2)
        go_ends()
        got_ends[me] = ends[me]

    def prefix():
        wait_ends()
        leap = leaps[me]

        def body(p, state):
            inits[p] = state
            return leap * state + got_ends[p]

        lax.fori_loop(0, n_ctx, body, jnp.zeros((1, 128), F32), unroll=4)
        go_inits()
        got_inits[me] = inits[me]

    def finish_conv():
        wait_inits()
        def one_group(q, _):
            lanes = lanes_of(q)
            decay = [jnp.exp(-row(rate_ref, r, lanes)) for r in range(modes)]
            coef = [row(coef_ref, r, lanes) for r in range(modes)]
            skip = row(skip_ref, 0, lanes)

            def second_pass(j, state):
                value = gated[j, :, lanes]
                after = tuple(decay[r] * state[r] + value for r in range(modes))
                terms = [coef[r] * after[r] for r in range(modes)] + [skip * value]
                while len(terms) > 1:
                    rest = terms[len(terms) // 2 * 2:]
                    terms = [a + b for a, b in zip(terms[::2], terms[1::2])] + rest
                hid[j, :, lanes] = query[j, :, lanes] * terms[0]
                return after

            begin = tuple(
                carry[r, :, lanes]
                + grow[r, :, lanes] * jnp.broadcast_to(got_inits[r * groups + q], (SUBS, 128))
                for r in range(modes)
            )
            lax.fori_loop(0, steps, second_pass, begin, unroll=2)
            return 0

        lax.fori_loop(0, groups, one_group, 0)
        hidb[...] = hid[...].reshape(steps * SUBS, chans).astype(BF16)

    herald(sem_r1, 1)
    first_pass(0)
    pl.semaphore_wait(sem_r1, 2)
    herald(sem_r2, 2)
    send_tail = remote(
        p_ref.at[:, pl.ds(rows - 8, 8)], tail, sem_tail.at[0], sem_tail.at[1],
        (lax.rem(me + 1, n_ctx), tp),
    )
    start(send_tail)
    ring_step(1)
    first_pass(1)
    pl.semaphore_wait(sem_r2, 2)
    herald(sem_r3, 4)
    first_pass(2)
    ring_step(2)
    first_pass(3)
    send_tail.wait_recv()
    lax.fori_loop(0, groups, first_steps, 0)
    pl.semaphore_wait(sem_r3, 2)
    herald(sem_r4, 1)
    ring_step(3)
    depart()
    for s in range(4, ring + 1):
        if s == first_wait:
            prefix()
        if s == second_wait:
            finish_conv()
        ring_step(s)
    if second_wait > ring:
        finish_conv()
    relay_bx(-ring)
    for e in range(nz):
        w_copy(hi, x + 2, z + e, sem_xbr, (e,), x_up).wait_recv()

    per = n_ctx // (2 * ny)

    def project(yy, cc):
        at = pl.multiple_of((yy * 2 + cc) * per, per)
        block = wall[pl.ds(at, per)].reshape(per * wrows, chans)
        return lax.dot_general(
            hidb[...], block, (((1,), (1,)), ((), ())), preferred_element_type=F32
        )

    def pair_copy(i):
        return remote(to_pair.at[i], from_pair.at[i], sem_pair.at[0, i], sem_pair.at[1, i], pair)

    def for_pair(i, _):
        to_pair[i] = project(lax.rem(y + 2 - i + ny, ny), 1 - core).astype(BF16)
        pair_copy(i).start()
        return 0

    def for_own(i, _):
        own[i] = project(lax.rem(y + 2 - i + ny, ny), core)
        return 0

    lax.fori_loop(0, ny, for_pair, 0)
    lax.fori_loop(0, ny, for_own, 0)
    pending.extend(pair_copy(i) for i in range(ny))

    def top(ref):
        return ref.at[pl.ds(0, half)]

    def bottom(ref):
        return ref.at[pl.ds(half, half)]

    def y_copy(src, dst, k, dev):
        return remote(src, dst, sem_y.at[0, k], sem_y.at[1, k], dev)

    far_up = y_copy(top(far), relay_up, 0, up)
    far_dn = y_copy(bottom(far), relay_dn, 1, dn)
    up_bottom = y_copy(bottom(fin_up), bottom(got_up), 2, up)
    dn_top = y_copy(top(fin_dn), top(got_dn), 3, dn)
    up_top = y_copy(top(fin_up), top(got_up), 4, up)
    dn_bottom = y_copy(bottom(fin_dn), bottom(got_dn), 5, dn)
    hi_rows, lo_rows = pl.ds(0, half), pl.ds(half, half)

    pair_copy(0).wait_recv()
    far[...] = (own[0] + from_pair[0].astype(F32)).astype(BF16)
    start(far_up)
    start(far_dn)
    pair_copy(1).wait_recv()
    fin_up[lo_rows] = (own[1, lo_rows] + from_pair[1, lo_rows].astype(F32)).astype(BF16)
    start(up_bottom)
    pair_copy(3).wait_recv()
    fin_dn[hi_rows] = (own[3, hi_rows] + from_pair[3, hi_rows].astype(F32)).astype(BF16)
    start(dn_top)
    far_up.wait_recv()
    fin_up[hi_rows] = (
        own[1, hi_rows] + from_pair[1, hi_rows].astype(F32) + relay_up[...].astype(F32)
    ).astype(BF16)
    start(up_top)
    far_dn.wait_recv()
    fin_dn[lo_rows] = (
        own[3, lo_rows] + from_pair[3, lo_rows].astype(F32) + relay_dn[...].astype(F32)
    ).astype(BF16)
    start(dn_bottom)
    pair_copy(2).wait_recv()
    own[2] = own[2] + from_pair[2].astype(F32)
    up_bottom.wait_recv()
    dn_top.wait_recv()
    up_top.wait_recv()
    dn_bottom.wait_recv()
    out_ref[...] = (own[2] + got_up[...].astype(F32) + got_dn[...].astype(F32)).astype(BF16)

    sent_ends()
    sent_inits()
    for copy in pending:
        copy.wait_send()


def per_device(dims, projected, short_filter, residues, rates, skip_gain, out_weight):
    nx, nz, ny = dims
    n_ctx = nx * nz
    rows, _, chans = projected.shape
    modes = rates.shape[1]
    steps = rows // SUBS
    groups = chans // 128
    wrows = out_weight.shape[1]
    rate_t = rates.T
    dma = pltpu.SemaphoreType.DMA
    vm = pltpu.VMEM
    ring = nz // 2
    out = pl.pallas_call(
        functools.partial(kernel, dims, FIRST, SECOND, SPLIT),
        out_shape=jax.ShapeDtypeStruct((rows, chans), BF16),
        in_specs=[pl.BlockSpec(memory_space=pltpu.HBM)] * 6,
        out_specs=pl.BlockSpec(memory_space=pltpu.VMEM),
        scratch_shapes=[
            vm((3, rows, chans), BF16),
            vm((3, 3, chans), F32),
            vm((modes, chans), F32),
            vm((modes, chans), F32),
            vm((1, chans), F32),
            vm((wrows, chans), BF16),
            vm((3, groups, rows + 8, 128), F32),
            vm((3, 8, chans), BF16),
            vm((modes, chans), F32),
            vm((n_ctx, 1, 128), F32),
            vm((steps, SUBS, chans), F32),
            vm((steps, SUBS, chans), F32),
            vm((modes, SUBS, chans), F32),
            vm((modes, SUBS, chans), F32),
            vm((steps, SUBS, chans), F32),
            vm((rows, chans), BF16),
            vm((n_ctx, 1, 128), F32),
            vm((n_ctx, 1, 128), F32),
            vm((n_ctx, 1, 128), F32),
            vm((n_ctx, 1, 128), F32),
            vm((n_ctx, wrows, chans), BF16),
            vm((ny, rows, chans), F32),
            vm((ny, rows, chans), BF16),
            vm((ny, rows, chans), BF16),
            vm((rows, chans), BF16),
            vm((rows // 2, chans), BF16),
            vm((rows // 2, chans), BF16),
            vm((rows, chans), BF16),
            vm((rows, chans), BF16),
            vm((rows, chans), BF16),
            vm((rows, chans), BF16),
            dma((2, n_ctx)),
            dma((2, n_ctx)),
            dma((2, nx)),
            dma((2, ring + 1, nx)),
            dma((2, ring + 1, nx)),
            dma((2, ring + 1)),
            dma((2, ring + 1)),
            dma((2, nz)),
            dma((2, nz)),
            dma((2, nz)),
            dma((7,)),
            dma((2, ny)),
            dma((2, 6)),
            dma((2,)),
            pltpu.SemaphoreType.REGULAR,
            pltpu.SemaphoreType.REGULAR,
            pltpu.SemaphoreType.REGULAR,
            pltpu.SemaphoreType.REGULAR,
        ],
        compiler_params=pltpu.CompilerParams(
            collective_id=0, has_side_effects=True, vmem_limit_bytes=67043328
        ),
    )(
        projected.transpose(1, 0, 2),
        short_filter,
        rate_t,
        residues.T,
        skip_gain[None, :],
        out_weight.T,
    )
    return out.reshape(steps, SUBS, chans).transpose(1, 0, 2).reshape(rows, chans)


def solution(mesh):
    dims = (4, mesh.shape["ctx"] // 4, mesh.shape["tp"] // 2)
    return jax.shard_map(
        functools.partial(per_device, dims),
        mesh=mesh,
        in_specs=(
            P("ctx", None, "tp"),
            P(None, None, "tp"),
            P("tp", None),
            P("tp", None),
            P("tp"),
            P("tp", "ctx"),
        ),
        out_specs=P("ctx", "tp"),
        check_vma=False,
    )
```

```python
import functools

import jax
import jax.numpy as jnp
from jax import lax
from jax.experimental import pallas as pl
from jax.experimental.pallas import tpu as pltpu
from jax.sharding import PartitionSpec as P

MESH = pl.DeviceIdType.MESH
F32 = jnp.float32
BF16 = jnp.bfloat16
SUBS = 8
FIRST, SECOND, SPLIT = 6, 9, 16


def kernel(
    dims, first_wait, second_wait, ra,
    p_in, taps_in, rate_in, res_in, skip_in, w_in,
    out_ref,
    p_ref, taps_ref, rate_ref, res_ref, skip_ref, w_ref,
    pf, tail, coef_ref, leaps, gated, query, carry, grow, hid, hidb,
    ends, got_ends, inits, got_inits,
    wall, own, to_pair, from_pair, far, relay_up, relay_dn,
    fin_up, fin_dn, got_up, got_dn,
    sem_e, sem_i, sem_xa, sem_zap, sem_zam, sem_zbp, sem_zbm,
    sem_xbp, sem_xbm, sem_xbr, sem_loc, sem_pair, sem_y, sem_tail,
    sem_r1, sem_r2, sem_r3, sem_r4,
):
    nx, nz, ny = dims
    n_ctx = nx * nz
    me = lax.axis_index("ctx")
    tp = lax.axis_index("tp")
    x, z = me // nz, me % nz
    y, core = tp // 2, tp % 2
    steps = p_ref.shape[1] // SUBS
    chans = p_ref.shape[2]
    modes = rate_ref.shape[0]
    groups = chans // 128
    half = 128
    wrows = w_ref.shape[0]

    def ctx_id(xx, zz):
        return (lax.rem(xx + nx, nx) * nz + lax.rem(zz + nz, nz), tp)

    def slot(xx, zz):
        return lax.rem(xx + nx, nx) * nz + lax.rem(zz + nz, nz)

    up = (me, lax.rem(y + 1, ny) * 2 + core)
    dn = (me, lax.rem(y + ny - 1, ny) * 2 + core)
    pair = (me, y * 2 + 1 - core)

    loads = [
        pltpu.make_async_copy(src, dst, sem_loc.at[i])
        for i, (src, dst) in enumerate((
            (w_in, w_ref), (p_in, p_ref), (taps_in, taps_ref), (rate_in, rate_ref),
            (res_in, res_ref), (skip_in, skip_ref), (w_in, wall.at[me]),
        ))
    ]
    for load in loads:
        load.start()

    barrier = pltpu.get_barrier_semaphore()

    near = [(lax.rem(x + dx, nx) * nz + z, tp) for dx in range(1, nx)]
    near += [(x * nz + lax.rem(z + dz, nz), tp) for dz in (1, nz - 1)]
    near += [up, dn, pair]
    for other in near:
        pl.semaphore_signal(barrier, inc=1, device_id=other, device_id_type=MESH)

    rows = steps * SUBS
    loads[0].wait()
    pl.semaphore_wait(barrier, len(near))

    pending = []

    def remote(src, dst, send, recv, dev):
        return pltpu.make_async_remote_copy(
            src_ref=src, dst_ref=dst, send_sem=send, recv_sem=recv,
            device_id=dev, device_id_type=MESH,
        )

    def exchange(src, dst, sems):
        def one(k):
            other = lax.rem(me + k, n_ctx)
            return remote(
                src.at[other], dst.at[me], sems.at[0, k], sems.at[1, k], (other, tp)
            )

        def come(k):
            other = lax.rem(me - k + n_ctx, n_ctx)
            return remote(
                src.at[other], dst.at[other], sems.at[0, k], sems.at[1, k], (other, tp)
            )

        def go(k, _):
            one(k).start()
            return 0

        def done(k, _):
            come(k).wait_recv()
            return 0

        def sent(k, _):
            one(k).wait_send()
            return 0

        return (
            lambda: lax.fori_loop(1, n_ctx, go, 0),
            lambda: lax.fori_loop(1, n_ctx, done, 0),
            lambda: lax.fori_loop(1, n_ctx, sent, 0),
        )

    lo, hi = pl.ds(0, ra), pl.ds(ra, wrows - ra)

    def w_copy(part, xx, zz, sems, idx, dev, own_src=False):
        at = wall.at[slot(xx, zz), part]
        src = w_ref.at[part] if own_src else at
        return remote(src, at, sems.at[(0, *idx)], sems.at[(1, *idx)], dev)

    def start(copy):
        copy.start()
        pending.append(copy)

    ring = nz // 2
    z_up, z_dn = ctx_id(x, z + 1), ctx_id(x, z - 1)
    x_up, x_dn = ctx_id(x + 1, z), ctx_id(x - 1, z)

    def send_ap(s, dx):
        start(w_copy(lo, x + dx, z - s + 1, sem_zap, (s, dx), z_up, s == 1 and dx == 0))

    def send_am(s, dx):
        start(w_copy(lo, x + dx, z + s - 1, sem_zam, (s, dx), z_dn, s == 1 and dx == 0))

    def send_bp(s):
        start(w_copy(hi, x, z - s + 1, sem_zbp, (s,), z_up, s == 1))

    def send_bm(s):
        start(w_copy(hi, x, z + s - 1, sem_zbm, (s,), z_dn, s == 1))

    def send_bx(e):
        start(w_copy(hi, x, z + e, sem_xbp, (e % nz,), x_up, e == 0))
        start(w_copy(hi, x, z + e, sem_xbm, (e % nz,), x_dn, e == 0))

    def relay_bx(e):
        w_copy(hi, x - 1, z + e, sem_xbp, (e % nz,), x_up).wait_recv()
        w_copy(hi, x + 1, z + e, sem_xbm, (e % nz,), x_dn).wait_recv()
        if e % 2 == 0:
            start(w_copy(hi, x - 1, z + e, sem_xbr, (e % nz,), x_up))
        else:
            start(w_copy(hi, x + 1, z + e, sem_xbr, (e % nz,), x_dn))

    send_ap(1, 0)
    send_am(1, 0)
    send_bp(1)
    send_bm(1)
    for dx in range(1, nx):
        start(w_copy(lo, x, z, sem_xa, (dx,), ctx_id(x + dx, z), True))
    send_bx(0)
    for dx in range(1, nx):
        w_copy(lo, x + dx, z, sem_xa, (nx - dx,), x_up).wait_recv()
        send_ap(1, dx)
        send_am(1, dx)

    def ring_step(s):
        w_copy(hi, x, z - s, sem_zbp, (s,), z_up).wait_recv()
        if s < ring:
            send_bp(s + 1)
        send_bx(-s)
        if s < ring:
            w_copy(hi, x, z + s, sem_zbm, (s,), z_dn).wait_recv()
            if s < ring - 1:
                send_bm(s + 1)
            send_bx(s)
        for dx in range(nx):
            w_copy(lo, x + dx, z - s, sem_zap, (s, dx), z_up).wait_recv()
            if s < ring:
                send_ap(s + 1, dx)
                w_copy(lo, x + dx, z + s, sem_zam, (s, dx), z_dn).wait_recv()
                if s < ring - 1:
                    send_am(s + 1, dx)
        if s > 1:
            relay_bx(-(s - 2))
        if s > 2:
            relay_bx(s - 2)

    go_ends, wait_ends, sent_ends = exchange(ends, got_ends, sem_e)
    go_inits, wait_inits, sent_inits = exchange(inits, got_inits, sem_i)


    def herald(sem, gap):
        for dz in (gap, nz - gap):
            pl.semaphore_signal(
                sem, inc=1, device_id=(x * nz + lax.rem(z + dz, nz), tp), device_id_type=MESH
            )

    def row(ref, at, lanes):
        return jnp.broadcast_to(ref[pl.ds(at, 1), lanes], (SUBS, 128))

    sub = lax.broadcasted_iota(jnp.int32, (SUBS, 128), 0)

    def lanes_of(q):
        return pl.ds(q * 128 if isinstance(q, int) else pl.multiple_of(q * 128, 128), 128)

    def mixer(q):
        lanes = lanes_of(q)
        taps = [
            [jnp.broadcast_to(taps_ref[i, pl.ds(s, 1), lanes], (SUBS, 128)) for i in range(3)]
            for s in range(3)
        ]

        def load(j):
            return tuple(pf[s, q, pl.ds(8 + j, SUBS, stride=steps), :] for s in range(3))

        def at_step(j, now, last, older):
            mixed = [
                taps[s][0] * now[s] + taps[s][1] * last[s] + taps[s][2] * older[s]
                for s in range(3)
            ]
            value = mixed[1] * mixed[2]
            gated[j, :, lanes] = value
            query[j, :, lanes] = mixed[0]
            return value

        return load, at_step

    def first_pass(q):
        lanes = pl.ds(q * 128, 128)
        decay = [jnp.exp(-row(rate_ref, r, lanes)) for r in range(modes)]
        load, at_step = mixer(q)

        def body(j, held):
            state, last, older = held
            now = load(j)
            value = at_step(j, now, last, older)
            return tuple(decay[r] * state[r] + value for r in range(modes)), now, last

        zero = jnp.zeros((SUBS, 128), F32)
        state, _, _ = lax.fori_loop(2, steps, body, ((zero,) * modes, load(1), load(0)), unroll=2)
        for r in range(modes):
            carry[r, :, lanes] = state[r]
            grow[r, :, lanes] = jnp.exp(
                -float(steps) * sub.astype(F32) * row(rate_ref, r, lanes)
            )

    def first_steps(q, _):
        lanes = lanes_of(q)
        for s in range(3):
            edge = tail[s, :, lanes].astype(F32)
            pf[s, q, pl.ds(0, 8), :] = jnp.where(me > 0, edge, 0.0)
        load, at_step = mixer(q)
        before = [load(j) for j in (-2, -1, 0, 1)]
        zeroth = at_step(0, before[2], before[1], before[0])
        first = at_step(1, before[3], before[2], before[1])
        for r in range(modes):
            rate = row(rate_ref, r, lanes)
            total = (
                carry[r, :, lanes]
                + jnp.exp(-float(steps - 1) * rate) * zeroth
                + jnp.exp(-float(steps - 2) * rate) * first
            )
            for gap in (1, 2, 4):
                moved = jnp.where(sub >= gap, pltpu.roll(total, gap, 0), 0.0)
                total = total + jnp.exp(-(float(steps * gap)) * rate) * moved
            ends[r * groups + q] = total[SUBS - 1:, :]
            leaps[r * groups + q] = jnp.exp(-float(rows) * rate[:1])
            carry[r, :, lanes] = jnp.where(sub >= 1, pltpu.roll(total, 1, 0), 0.0)
        return 0

    def depart():
        pl.semaphore_wait(sem_r4, 2)
        go_ends()
        got_ends[me] = ends[me]

    def prefix():
        wait_ends()
        leap = leaps[me]

        def body(p, state):
            inits[p] = state
            return leap * state + got_ends[p]

        lax.fori_loop(0, n_ctx, body, jnp.zeros((1, 128), F32), unroll=4)
        go_inits()
        got_inits[me] = inits[me]

    def finish_conv():
        wait_inits()
        def one_group(q, _):
            lanes = lanes_of(q)
            decay = [jnp.exp(-row(rate_ref, r, lanes)) for r in range(modes)]
            coef = [row(coef_ref, r, lanes) for r in range(modes)]
            skip = row(skip_ref, 0, lanes)

            def second_pass(j, state):
                value = gated[j, :, lanes]
                after = tuple(decay[r] * state[r] + value for r in range(modes))
                terms = [coef[r] * after[r] for r in range(modes)] + [skip * value]
                while len(terms) > 1:
                    rest = terms[len(terms) // 2 * 2:]
                    terms = [a + b for a, b in zip(terms[::2], terms[1::2])] + rest
                hid[j, :, lanes] = query[j, :, lanes] * terms[0]
                return after

            begin = tuple(
                carry[r, :, lanes]
                + grow[r, :, lanes] * jnp.broadcast_to(got_inits[r * groups + q], (SUBS, 128))
                for r in range(modes)
            )
            lax.fori_loop(0, steps, second_pass, begin, unroll=2)
            return 0

        lax.fori_loop(0, groups, one_group, 0)
        hidb[...] = hid[...].reshape(steps * SUBS, chans).astype(BF16)

    herald(sem_r1, 1)
    for load in loads[1:]:
        load.wait()
    twice = 2.0 * rate_ref[...]
    small = jnp.ones_like(twice)
    for k in range(9, 1, -1):
        small = 1.0 - small * twice * (1.0 / k)
    lost = jnp.where(twice < 0.25, twice * small, 1.0 - jnp.exp(-twice))
    coef_ref[...] = res_ref[...] * jnp.sqrt(lost)
    for s in range(3):
        for q in range(groups):
            pf[s, q, pl.ds(8, rows), :] = p_ref[s, :, pl.ds(q * 128, 128)].astype(F32)

    first_pass(0)
    pl.semaphore_wait(sem_r1, 2)
    herald(sem_r2, 2)
    send_tail = remote(
        p_ref.at[:, pl.ds(rows - 8, 8)], tail, sem_tail.at[0], sem_tail.at[1],
        (lax.rem(me + 1, n_ctx), tp),
    )
    start(send_tail)
    ring_step(1)
    first_pass(1)
    pl.semaphore_wait(sem_r2, 2)
    herald(sem_r3, 4)
    first_pass(2)
    ring_step(2)
    first_pass(3)
    send_tail.wait_recv()
    lax.fori_loop(0, groups, first_steps, 0)
    pl.semaphore_wait(sem_r3, 2)
    herald(sem_r4, 1)
    ring_step(3)
    depart()
    for s in range(4, ring + 1):
        if s == first_wait:
            prefix()
        if s == second_wait:
            finish_conv()
        ring_step(s)
    if second_wait > ring:
        finish_conv()
    relay_bx(1 - ring)
    relay_bx(ring - 1)
    relay_bx(-ring)
    for e in range(nz):
        w_copy(hi, x + 2, z + e, sem_xbr, (e,), x_up).wait_recv()

    per = n_ctx // (2 * ny)

    def project(yy, cc):
        at = pl.multiple_of((yy * 2 + cc) * per, per)
        block = wall[pl.ds(at, per)].reshape(per * wrows, chans)
        return lax.dot_general(
            hidb[...], block, (((1,), (1,)), ((), ())), preferred_element_type=F32
        )

    def pair_copy(i):
        return remote(to_pair.at[i], from_pair.at[i], sem_pair.at[0, i], sem_pair.at[1, i], pair)

    def for_pair(i, _):
        to_pair[i] = project(lax.rem(y + 2 - i + ny, ny), 1 - core).astype(BF16)
        pair_copy(i).start()
        return 0

    def for_own(i, _):
        own[i] = project(lax.rem(y + 2 - i + ny, ny), core)
        return 0

    lax.fori_loop(0, ny, for_pair, 0)
    lax.fori_loop(0, ny, for_own, 0)
    pending.extend(pair_copy(i) for i in range(ny))

    def top(ref):
        return ref.at[pl.ds(0, half)]

    def bottom(ref):
        return ref.at[pl.ds(half, half)]

    def y_copy(src, dst, k, dev):
        return remote(src, dst, sem_y.at[0, k], sem_y.at[1, k], dev)

    far_up = y_copy(top(far), relay_up, 0, up)
    far_dn = y_copy(bottom(far), relay_dn, 1, dn)
    up_bottom = y_copy(bottom(fin_up), bottom(got_up), 2, up)
    dn_top = y_copy(top(fin_dn), top(got_dn), 3, dn)
    up_top = y_copy(top(fin_up), top(got_up), 4, up)
    dn_bottom = y_copy(bottom(fin_dn), bottom(got_dn), 5, dn)
    hi_rows, lo_rows = pl.ds(0, half), pl.ds(half, half)

    pair_copy(0).wait_recv()
    far[...] = (own[0] + from_pair[0].astype(F32)).astype(BF16)
    start(far_up)
    start(far_dn)
    pair_copy(1).wait_recv()
    fin_up[lo_rows] = (own[1, lo_rows] + from_pair[1, lo_rows].astype(F32)).astype(BF16)
    start(up_bottom)
    pair_copy(3).wait_recv()
    fin_dn[hi_rows] = (own[3, hi_rows] + from_pair[3, hi_rows].astype(F32)).astype(BF16)
    start(dn_top)
    far_up.wait_recv()
    fin_up[hi_rows] = (
        own[1, hi_rows] + from_pair[1, hi_rows].astype(F32) + relay_up[...].astype(F32)
    ).astype(BF16)
    start(up_top)
    far_dn.wait_recv()
    fin_dn[lo_rows] = (
        own[3, lo_rows] + from_pair[3, lo_rows].astype(F32) + relay_dn[...].astype(F32)
    ).astype(BF16)
    start(dn_bottom)
    pair_copy(2).wait_recv()
    own[2] = own[2] + from_pair[2].astype(F32)
    up_bottom.wait_recv()
    dn_top.wait_recv()
    up_top.wait_recv()
    dn_bottom.wait_recv()
    out_ref[...] = (own[2] + got_up[...].astype(F32) + got_dn[...].astype(F32)).astype(BF16)

    sent_ends()
    sent_inits()
    for copy in pending:
        copy.wait_send()


def per_device(dims, projected, short_filter, residues, rates, skip_gain, out_weight):
    nx, nz, ny = dims
    n_ctx = nx * nz
    rows, _, chans = projected.shape
    modes = rates.shape[1]
    steps = rows // SUBS
    groups = chans // 128
    wrows = out_weight.shape[1]
    rate_t = rates.T
    dma = pltpu.SemaphoreType.DMA
    vm = pltpu.VMEM
    ring = nz // 2
    out = pl.pallas_call(
        functools.partial(kernel, dims, FIRST, SECOND, SPLIT),
        out_shape=jax.ShapeDtypeStruct((rows, chans), BF16),
        in_specs=[pl.BlockSpec(memory_space=pltpu.HBM)] * 6,
        out_specs=pl.BlockSpec(memory_space=pltpu.VMEM),
        scratch_shapes=[
            vm((3, rows, chans), BF16),
            vm((3, 3, chans), F32),
            vm((modes, chans), F32),
            vm((modes, chans), F32),
            vm((1, chans), F32),
            vm((wrows, chans), BF16),
            vm((3, groups, rows + 8, 128), F32),
            vm((3, 8, chans), BF16),
            vm((modes, chans), F32),
            vm((n_ctx, 1, 128), F32),
            vm((steps, SUBS, chans), F32),
            vm((steps, SUBS, chans), F32),
            vm((modes, SUBS, chans), F32),
            vm((modes, SUBS, chans), F32),
            vm((steps, SUBS, chans), F32),
            vm((rows, chans), BF16),
            vm((n_ctx, 1, 128), F32),
            vm((n_ctx, 1, 128), F32),
            vm((n_ctx, 1, 128), F32),
            vm((n_ctx, 1, 128), F32),
            vm((n_ctx, wrows, chans), BF16),
            vm((ny, rows, chans), F32),
            vm((ny, rows, chans), BF16),
            vm((ny, rows, chans), BF16),
            vm((rows, chans), BF16),
            vm((rows // 2, chans), BF16),
            vm((rows // 2, chans), BF16),
            vm((rows, chans), BF16),
            vm((rows, chans), BF16),
            vm((rows, chans), BF16),
            vm((rows, chans), BF16),
            dma((2, n_ctx)),
            dma((2, n_ctx)),
            dma((2, nx)),
            dma((2, ring + 1, nx)),
            dma((2, ring + 1, nx)),
            dma((2, ring + 1)),
            dma((2, ring + 1)),
            dma((2, nz)),
            dma((2, nz)),
            dma((2, nz)),
            dma((7,)),
            dma((2, ny)),
            dma((2, 6)),
            dma((2,)),
            pltpu.SemaphoreType.REGULAR,
            pltpu.SemaphoreType.REGULAR,
            pltpu.SemaphoreType.REGULAR,
            pltpu.SemaphoreType.REGULAR,
        ],
        compiler_params=pltpu.CompilerParams(
            collective_id=0, has_side_effects=True, vmem_limit_bytes=67043328
        ),
    )(
        projected.transpose(1, 0, 2),
        short_filter,
        rate_t,
        residues.T,
        skip_gain[None, :],
        out_weight.T,
    )
    return out.reshape(steps, SUBS, chans).transpose(1, 0, 2).reshape(rows, chans)


def solution(mesh):
    dims = (4, mesh.shape["ctx"] // 4, mesh.shape["tp"] // 2)
    return jax.shard_map(
        functools.partial(per_device, dims),
        mesh=mesh,
        in_specs=(
            P("ctx", None, "tp"),
            P(None, None, "tp"),
            P("tp", None),
            P("tp", None),
            P("tp"),
            P("tp", "ctx"),
        ),
        out_specs=P("ctx", "tp"),
        check_vma=False,
    )
```
